256 devices in a mesh: cols: 32 (over z_lo, x, core), spec: 8 (over y, z_hi).
Axes of the slice: x: 4, y: 4, z: 8 (z_hi: 2, z_lo: 4; z = z_hi * 4 + z_lo), core: 2. Of those that a mesh axis runs over, the one named last changes fastest.
Arguments:
- air_state: float32 [8, 512, 256, 128], P(None, 'cols', 'spec'), may hold values from -13 to 13, as said below
- courant_x: float32 [128], replicated, may hold values from -0.45 to 0.45
- courant_y: float32 [128], replicated, may hold values from -0.45 to 0.45
- cos_zenith: float32 [512, 256], P('cols', 'spec'), may hold values from 0.15 to 1
- sun_index: int32 [32, 8, 96], P('cols', 'spec'), may hold values from 0 to 511, as said below
- sun_count: int32 [8, 32], replicated, may hold values from 1 to 96, 768 in all within a row
- in_weight: bfloat16 [7, 128], replicated, may hold values from -3 to 3
- in_bias: float32 [128], replicated, may hold values from -4 to 4
- mid_weight: bfloat16 [128, 128], replicated, may hold values from -0.099609375 to 0.099609375
- mid_bias: float32 [128], replicated, may hold values from -2 to 2
- out_weight: bfloat16 [128, 256, 128], P(None, 'spec'), may hold values from -0.5 to 0.5
- out_bias: float32 [256], P('spec'), may hold values from -3 to 3
- absorption: float32 [256], P('spec'), may hold values from 0.00390625 to 0.0625
- solar_flux: float32 [256], P('spec'), may hold values from 0.03 to 1
Outputs:
- new_state: float32 [8, 512, 256, 128], P(None, 'cols', 'spec')
- solar_heating: float32 [512, 256, 128], P('cols', 'spec')
The draws below stay inside these ranges and needn't reach their ends.
Inputs may be any that keep to these rules, and one draw needn't show every extreme that they name: For each tile (c, s) the entries sun_index[c, s, :] are distinct cell numbers m of that tile, naming the grid column (c * 16 + m // 32, s * 32 + m % 32); only the first sun_count[s, c] of them are sunlit, the others are unused. `sun_count`: entry [s, c] is the number of sunlit columns of tile (c, s); every row sums to exactly 768, and one entry of each row equals 96. `air_state`: the fields' values.
All inputs are finite; a program needn't handle non-finite values.
Results may differ from the reference program's by a relative error of at most 0.0023.
Values may be sent and summed in bfloat16 or wider, within the bound.
No kernel may reach another device: no remote copies, remote signals or barrier semaphores. Data moves between devices by JAX's collectives and lax.ppermute only.
A program may use at most 64 MiB of HBM per device.

```python
import math
import jax
import jax.numpy as jnp
import numpy as np
from jax import lax

F = 8
NIN = 7
L = 128
HID = 128
G = 256
SECTIONS = 4
CX = 16
CY = 32
SUN_MAX = 96
SUN_MEAN = 24
GX = 32
GY = 8
NX = 512
NY = 256


def draw_sun_index(key, part):
    tile_keys = jax.random.split(key, GX * GY)

    def pick_cells(tile_key):
        return jax.random.permutation(tile_key, CX * CY)[:SUN_MAX]
    chosen = jax.vmap(pick_cells)(tile_keys)
    return chosen.reshape(GX, GY, SUN_MAX).astype(jnp.int32)


def draw_air_state(key, part):
    base_key, scale_key, offset_key = jax.random.split(jax.random.fold_in(key, 7), 3)
    base = jnp.clip(jax.random.normal(base_key, (F, NX, NY, L), jnp.float32), -4.0, 4.0)
    offset_span = 1.0
    column_scale = jnp.exp(jax.random.uniform(scale_key, (F, NX, NY, 1), jnp.float32, -1.5, 1.0))
    tile_offset = jax.random.uniform(offset_key, (F, GX, GY), jnp.float32, -offset_span, offset_span)
    spread_offset = jnp.repeat(jnp.repeat(tile_offset, CX, axis=1), CY, axis=2)[:, :, :, None]
    return (base * column_scale + spread_offset).astype(jnp.float32)


def shard_levels(stream_key, extent, cuts, smallest, top_value):
    def one(axis_at, shards_of):
        steps = jax.random.uniform(jax.random.fold_in(jax.random.fold_in(stream_key, 6), axis_at), (shards_of,), jnp.float32, smallest / len(cuts), top_value / len(cuts))
        return jnp.repeat(jnp.exp(steps), extent[axis_at] // shards_of).reshape((-1,) + (1,) * (len(extent) - axis_at - 1))

    level = one(*cuts[0])
    for cut in cuts[1:]:
        level = level * one(*cut)
    return level


def profile(amount, total, limit, skew):
    portions = [(1 << 20) // math.isqrt(grade ** skew) + 1 for grade in range(2, amount + 1)]
    surplus, given = total - limit - (amount - 1), [1] * (amount - 1)
    while surplus > 0:
        free = [i for i in range(amount - 1) if given[i] < limit]
        mass, budget = sum([portions[i] for i in free]), surplus
        for i in free:
            more = min(limit - given[i], max(1, budget * portions[i] // mass), surplus)
            given[i] = given[i] + more
            surplus = surplus - more
    return np.array([limit] + given)


def ragged(stream_key, number_of, total, limit, skew):
    if number_of == 2:
        one = jax.random.randint(stream_key, (), max(1, total - limit), min(limit, total - 1) + 1)
        return jnp.stack([one, total - one])
    tallies = jnp.asarray(profile(number_of, total, limit, skew), jnp.int32)
    twos = (number_of - 1) // 2
    source_of, sink = tallies[1:1 + 2 * twos:2], tallies[2:2 + 2 * twos:2]
    room = jnp.minimum(source_of - 1, limit - sink)
    passed = jax.random.randint(jax.random.fold_in(stream_key, 1), (twos,), 0, 1 << 20) % (room + 1)
    tallies = tallies.at[1:1 + 2 * twos:2].set(source_of - passed).at[2:2 + 2 * twos:2].set(sink + passed)
    return tallies[jax.random.permutation(jax.random.fold_in(stream_key, 2), number_of)]


def normal_values(rng, extent, scale, limit, pieces=(), kind=jnp.bfloat16):
    drawn = jax.random.normal(rng, extent, jnp.float32) * scale
    if len(pieces) > 0:
        drawn = shard_levels(rng, extent, pieces, -0.22, 0.18) * drawn
    return jnp.clip(drawn, min=-limit, max=limit).astype(kind)


def setup_inputs(seed: int = 0) -> dict:
    keys = jax.random.split(jax.random.key(seed), 15)
    return {
        "air_state": draw_air_state(jax.random.fold_in(keys[14], 71), 0),
        "courant_x": jnp.clip(jax.random.uniform(keys[1], (L,), jnp.float32, -0.45, 0.45), -0.45, 0.45),
        "courant_y": jnp.clip(jax.random.uniform(keys[2], (L,), jnp.float32, -0.45, 0.45), -0.45, 0.45),
        "cos_zenith": jnp.clip(0.15 + 0.85 * jax.random.uniform(keys[3], (NX, NY), jnp.float32) ** shard_levels(keys[3], (NX, NY), ((0, 32), (1, 8)), -0.2, 0.2), 0.15, 1.0),
        "sun_index": draw_sun_index(jax.random.fold_in(keys[14], 71), 0),
        "sun_count": jax.vmap(lambda own: ragged(own, GX, SUN_MEAN * GX, SUN_MAX, 2))(jax.random.split(keys[5], GY)).reshape((GY, GX)).astype(jnp.int32),
        "in_weight": jnp.clip(jax.random.uniform(keys[6], (NIN, HID), jnp.float32, -3.0, 3.0), -3.0, 3.0).astype(jnp.bfloat16),
        "in_bias": jnp.clip(jax.random.uniform(keys[7], (HID,), jnp.float32, -4.0, 4.0), -4.0, 4.0),
        "mid_weight": jnp.clip(jax.random.uniform(keys[8], (HID, HID), jnp.float32, -0.099609375, 0.099609375), -0.099609375, 0.099609375).astype(jnp.bfloat16),
        "mid_bias": jnp.clip(jax.random.uniform(keys[9], (HID,), jnp.float32, -2.0, 2.0), -2.0, 2.0),
        "out_weight": normal_values(keys[10], (L, G, HID), HID ** -0.5, 0.5, ((1, 8),)),
        "out_bias": normal_values(keys[11], (G,), 0.5, 3.0, ((0, 8),), jnp.float32),
        "absorption": jnp.clip(jnp.exp(math.log(0.0625) - 2.7725887 * jax.random.uniform(keys[12], (G,), jnp.float32) ** shard_levels(keys[12], (G,), ((0, 8),), -0.2, 0.2)), 0.00390625, 0.0625),
        "solar_flux": jnp.clip(jnp.exp(math.log(1.0) - 3.506558 * jax.random.uniform(keys[13], (G,), jnp.float32) ** shard_levels(keys[13], (G,), ((0, 8),), -0.2, 0.2)), 0.03, 1.0),
    }


DIFFUSION = 0.05
ALBEDO = 0.3
DIFFUSIVITY = 1.66


def advect(current, courant_x, courant_y):
    eastern = jnp.roll(current, -1, axis=1)
    western = jnp.roll(current, 1, axis=1)
    northern = jnp.roll(current, -1, axis=2)
    southern = jnp.roll(current, 1, axis=2)
    return (current - 0.5 * courant_x * (eastern - western)
            + (0.5 * courant_x * courant_x + DIFFUSION) * (eastern - 2.0 * current + western)
            - 0.5 * courant_y * (northern - southern)
            + (0.5 * courant_y * courant_y + DIFFUSION) * (northern - 2.0 * current + southern))


def radiate(features, slant_cos, in_weight, in_bias, mid_weight, mid_bias, out_weight, out_bias, absorption, solar_flux):
    features = lax.optimization_barrier(features)
    inputs = jnp.transpose(features, (2, 0, 1)).astype(jnp.float32)
    first_sum = jnp.einsum("lni,ih->lnh", inputs, in_weight.astype(jnp.float32))
    hidden_one = lax.optimization_barrier(jax.nn.silu(first_sum + in_bias).astype(jnp.bfloat16))
    second = jnp.einsum("lnh,hk->lnk", hidden_one.astype(jnp.float32), mid_weight.astype(jnp.float32))
    hidden_two = lax.optimization_barrier(jax.nn.silu(second + mid_bias).astype(jnp.bfloat16))
    logits = jnp.einsum("lgh,lnh->lgn", out_weight.astype(jnp.float32), hidden_two.astype(jnp.float32))
    depth_layer = absorption[:, None] * jax.nn.softplus(logits + out_bias[:, None])
    optical_depth = jnp.cumsum(depth_layer, axis=0)
    cosine = slant_cos.astype(jnp.float32)[None, None, :]
    column_total = optical_depth[-1:]
    source = solar_flux[None, :, None] * cosine
    down_top = source * jnp.exp(-(optical_depth - depth_layer) / cosine)
    down_bottom = source * jnp.exp(-optical_depth / cosine)
    up_base = ALBEDO * source * jnp.exp(-column_total / cosine)
    up_top = up_base * jnp.exp(-DIFFUSIVITY * (column_total - optical_depth + depth_layer))
    up_bottom = up_base * jnp.exp(-DIFFUSIVITY * (column_total - optical_depth))
    absorbed = down_top - down_bottom + up_bottom - up_top
    return jnp.transpose(jnp.sum(absorbed, axis=1))


def reference(air_state, courant_x, courant_y, cos_zenith, sun_index, sun_count, in_weight, in_bias, mid_weight, mid_bias, out_weight, out_bias, absorption, solar_flux):
    current = air_state
    for section_number in range(SECTIONS):
        current = advect(current, courant_x, courant_y)
    counts = jnp.transpose(sun_count).reshape(-1).astype(jnp.int32)
    count_ends = jnp.cumsum(counts).astype(jnp.int32)
    starts = count_ends - counts
    sunlit_total = SUN_MEAN * GX * GY
    rank_list = jnp.arange(sunlit_total, dtype=jnp.int32)
    tile_number = jnp.searchsorted(count_ends, rank_list, side="right").astype(jnp.int32)
    within = rank_list - starts[tile_number]
    tile_x = tile_number // GY
    tile_y = tile_number % GY
    cell_number = sun_index[tile_x, tile_y, within]
    cell_x = tile_x * CX + cell_number // CY
    cell_y = tile_y * CY + cell_number % CY
    features = jnp.transpose(air_state[:NIN][:, cell_x, cell_y, :], (1, 0, 2)).astype(jnp.bfloat16)
    slant_cos = cos_zenith[cell_x, cell_y].astype(jnp.bfloat16)
    block_rows = math.gcd(sunlit_total, 128)
    count_blocks = sunlit_total // block_rows
    shaped = (features.reshape(count_blocks, block_rows, NIN, L), slant_cos.reshape(count_blocks, block_rows))

    def one_block(block_pair):
        return radiate(block_pair[0], block_pair[1], in_weight, in_bias, mid_weight, mid_bias, out_weight, out_bias, absorption, solar_flux)

    heating = lax.map(one_block, shaped).reshape(sunlit_total, L)
    heat_grid = jnp.zeros((NX, NY, L), jnp.float32).at[cell_x, cell_y].add(heating)
    new_state = current.at[0].add(heat_grid)
    return (new_state, heat_grid)
```

```python
import functools

import jax
import jax.numpy as jnp
from jax import lax
from jax.experimental import pallas as pl
from jax.experimental.pallas import tpu as pltpu
from jax.sharding import PartitionSpec as P

NIN = 7
SECTIONS = 4
WIDE = 4
DIFFUSION = 0.05
ALBEDO = 0.3
DIFFUSIVITY = 1.66
LANES = 128
VMEM_LIMIT = 60 * 1024 * 1024

F32 = jnp.float32
BF16 = jnp.bfloat16


def vmem():
    return pl.BlockSpec(memory_space=pltpu.VMEM)


def smem():
    return pl.BlockSpec(memory_space=pltpu.SMEM)


def params(**more):
    return pltpu.CompilerParams(vmem_limit_bytes=VMEM_LIMIT, **more)


def gather_kernel(cells, width_x, width_y, index_ref, cos_ref, state_ref, feat_ref, xlo_ref, xhi_ref, ylo_ref, yhi_ref):
    fields = state_ref.shape[0] // cells
    last = lax.broadcasted_iota(jnp.int32, (fields, LANES), 0) == NIN

    def one(j, carry):
        m = index_ref[j]
        rows = state_ref[pl.ds(m, fields, stride=cells), :]
        feat_ref[j] = jnp.where(last, cos_ref[m], rows).astype(BF16)
        return carry

    lax.fori_loop(0, feat_ref.shape[0], one, 0, unroll=8)
    for f in range(fields):
        for w in range(WIDE):
            xlo_ref[f, w] = state_ref[pl.ds(f * cells + w * width_y, width_y), :].astype(BF16)
            xhi_ref[f, w] = state_ref[pl.ds(f * cells + (width_x - WIDE + w) * width_y, width_y), :].astype(BF16)
            ylo_ref[f, w] = state_ref[pl.ds(f * cells + w, width_x, stride=width_y), :].astype(BF16)
            yhi_ref[f, w] = state_ref[pl.ds(f * cells + width_y - WIDE + w, width_x, stride=width_y), :].astype(BF16)


def edge_kernel(ylo_ref, yhi_ref, xlo_ref, xhi_ref, mlo_ref, mhi_ref, buf):
    width_y = xlo_ref.shape[2]
    for f in range(ylo_ref.shape[0]):
        for w in range(WIDE):
            buf[pl.ds(w * width_y, width_y), :] = xhi_ref[f, w].astype(F32)
            buf[pl.ds((WIDE + w) * width_y, width_y), :] = xlo_ref[f, w].astype(F32)
        for w in range(WIDE):
            for src, dst, row in ((ylo_ref, mlo_ref, w), (yhi_ref, mhi_ref, width_y - WIDE + w)):
                corner = buf[pl.ds(row, 2 * WIDE, stride=width_y), :]
                dst[f, w] = jnp.concatenate([src[f, w].astype(F32), corner], axis=0).astype(BF16)


def advect_kernel(width_x, width_y, state_ref, xlo_ref, xhi_ref, ylo_ref, yhi_ref, coef_ref, out_ref, one, two):
    ring_x, ring_y = width_x + 2 * WIDE, width_y + 2 * WIDE
    for x in range(width_x):
        one[pl.ds(x * ring_y, width_y), :] = state_ref[0, pl.ds(x * width_y, width_y), :]
    for w in range(WIDE):
        one[pl.ds((width_x + w) * ring_y, width_y), :] = xhi_ref[0, w].astype(F32)
        one[pl.ds((width_x + WIDE + w) * ring_y, width_y), :] = xlo_ref[0, w].astype(F32)
        one[pl.ds(width_y + w, ring_x, stride=ring_y), :] = yhi_ref[0, w].astype(F32)
        one[pl.ds(width_y + WIDE + w, ring_x, stride=ring_y), :] = ylo_ref[0, w].astype(F32)
    centre, east, west, north, south = (coef_ref[pl.ds(k, 1), :] for k in range(5))
    src, dst = one, two
    for section in range(SECTIONS):
        left = WIDE - 1 - section
        wanted = list(range(width_x + left)) + list(range(ring_x - left, ring_x))
        for x in wanted:
            q = src[pl.ds(x * ring_y, ring_y), :]
            e = src[pl.ds(((x + 1) % ring_x) * ring_y, ring_y), :]
            w = src[pl.ds(((x - 1) % ring_x) * ring_y, ring_y), :]
            n = pltpu.roll(q, ring_y - 1, 0)
            s = pltpu.roll(q, 1, 0)
            new = centre * q + east * e + west * w + north * n + south * s
            if section == SECTIONS - 1:
                out_ref[0, pl.ds(x * width_y, width_y), :] = new[:width_y]
            else:
                dst[pl.ds(x * ring_y, ring_y), :] = new
        src, dst = dst, src


def radiate_kernel(
    count_ref,
    mine_ref,
    theirs_ref,
    first_ref,
    first_bias_ref,
    mid_ref,
    mid_bias_ref,
    outa_ref,
    outb_ref,
    out_bias_ref,
    absorb_ref,
    flux_ref,
    heat_mine_ref,
    heat_theirs_ref,
    packed,
    grouped,
    depths,
    sums,
    heats,
):
    capacity = mine_ref.shape[0] // 2
    levels = outa_ref.shape[0]
    points = absorb_ref.shape[0]
    fields = mine_ref.shape[1]
    group_levels = LANES // fields
    groups = levels // group_levels
    sources = ((mine_ref, 0), (mine_ref, capacity), (theirs_ref, 0), (theirs_ref, capacity))
    offset = jnp.int32(0)
    offsets = []
    for t, (ref, base) in enumerate(sources):
        offsets.append(offset)

        def pack(i, carry, ref=ref, base=base, offset=offset):
            packed[pl.ds((offset + i) * fields, fields), :] = ref[base + i].astype(F32)
            return carry

        lax.fori_loop(0, count_ref[t], pack, 0)
        offset = offset + count_ref[t]
    lane = lax.broadcasted_iota(jnp.int32, (16, LANES), 1) // group_levels

    def chunk(q, carry):
        first_row = q * LANES

        def regroup(r, carry2):
            base = (first_row + r * 16) * fields
            rows = [packed[pl.ds(base + f, 16, stride=fields), :] for f in range(fields)]
            for g in range(groups):
                made = rows[0] if g == 0 else pltpu.roll(rows[0], (-g * group_levels) % LANES, 1)
                for f in range(1, fields):
                    shift = ((f - g) * group_levels) % LANES
                    moved = rows[f] if shift == 0 else pltpu.roll(rows[f], shift, 1)
                    made = jnp.where(lane == f, moved, made)
                grouped[g, pl.ds(pl.multiple_of(r * 16, 16), 16), :] = made.astype(BF16)
            return carry2

        lax.fori_loop(0, LANES // 16, regroup, 0)
        slant_rows = packed[pl.ds(first_row * fields + NIN, LANES, stride=fields), :]
        cosine = jnp.transpose(slant_rows)[:8, :]

        def pair(i, depth):
            g = i // (group_levels // 2)
            p = i % (group_levels // 2)
            u = jnp.dot(grouped[g], first_ref[p], preferred_element_type=F32) + first_bias_ref[...]
            hidden_one = (u + u * jnp.tanh(u)).astype(BF16)
            v = jnp.dot(hidden_one, mid_ref[...], preferred_element_type=F32) + mid_bias_ref[...]
            hidden_two = (v + v * jnp.tanh(v)).astype(BF16)
            for j in range(2):
                level = 2 * i + j
                weight = jnp.concatenate([outa_ref[level], outb_ref[level]], axis=0)
                logits = lax.dot_general(
                    weight,
                    hidden_two[:, j * LANES : (j + 1) * LANES],
                    (((1,), (1,)), ((), ())),
                    preferred_element_type=F32,
                )
                logits = logits + out_bias_ref[...]
                soft = jnp.maximum(logits, 0.0) + jnp.log(1.0 + jnp.exp(-jnp.abs(logits)))
                depth = depth + absorb_ref[...] * soft
                depths[level] = depth
            return depth

        total = lax.fori_loop(0, levels // 2, pair, jnp.zeros((points, LANES), F32))
        wide = jnp.tile(cosine, (points // 8, 1))
        steep = -1.0 / wide
        source = flux_ref[...] * wide
        base = ALBEDO * source * jnp.exp(total * steep)
        before = source - base * jnp.exp(-DIFFUSIVITY * total)

        def level_heat(level, before):
            depth = depths[level]
            now = source * jnp.exp(depth * steep) - base * jnp.exp(DIFFUSIVITY * (depth - total))
            lost = before - now
            sums[pl.ds(pl.multiple_of(level * 8, 8), 8), :] = jnp.sum(lost.reshape(points // 8, 8, LANES), axis=0)
            return now

        lax.fori_loop(0, levels, level_heat, before, unroll=2)
        heat = sums[pl.ds(0, levels, stride=8), :]
        for k in range(1, 8):
            heat = heat + sums[pl.ds(k, levels, stride=8), :]
        heats[pl.ds(pl.multiple_of(first_row, LANES), LANES), :] = jnp.transpose(heat)
        return carry

    lax.fori_loop(0, (offset + LANES - 1) // LANES, chunk, 0)
    for t, (ref, base) in enumerate(
        ((heat_mine_ref, 0), (heat_mine_ref, capacity), (heat_theirs_ref, 0), (heat_theirs_ref, capacity))
    ):

        def unpack(i, carry, ref=ref, base=base, offset=offsets[t]):
            ref[pl.ds(base + i, 1), :] = heats[pl.ds(offset + i, 1), :]
            return carry

        lax.fori_loop(0, count_ref[t], unpack, 0)


def finish_kernel(index_ref, count_ref, heat_a, heat_b, state_in, state_out, grid_ref, plane, sems):
    fetch = pltpu.make_async_copy(state_in.at[0], plane, sems.at[0])
    fetch.start()
    grid_ref[...] = jnp.zeros_like(grid_ref)

    def one(j, carry):
        grid_ref[pl.ds(index_ref[j], 1), :] = heat_a[pl.ds(j, 1), :] + heat_b[pl.ds(j, 1), :]
        return carry

    lax.fori_loop(0, count_ref[0], one, 0)
    fetch.wait()
    plane[...] = plane[...] + grid_ref[...]
    store = pltpu.make_async_copy(plane, state_out.at[0], sems.at[1])
    store.start()
    store.wait()


def on_device(
    air_state,
    courant_x,
    courant_y,
    cos_zenith,
    sun_index,
    sun_count,
    in_weight,
    in_bias,
    mid_weight,
    mid_bias,
    out_weight,
    out_bias,
    absorption,
    solar_flux,
):
    fields, width_x, width_y, levels = air_state.shape
    cells = width_x * width_y
    capacity = sun_index.shape[-1]
    hidden = mid_weight.shape[0]
    points = out_weight.shape[1]
    cols, spec = lax.axis_size("cols"), lax.axis_size("spec")
    plane_cols = cols // 4

    def mirrored(c):
        return (3 - c // plane_cols) * plane_cols + c % plane_cols

    def both(target):
        return [(c * spec + s, (lambda d: d[0] * spec + d[1])(target(c, s))) for c in range(cols) for s in range(spec)]

    def send(value, target):
        return lax.ppermute(value, ("cols", "spec"), both(target))

    def to_z(c, s):
        return mirrored(c), s ^ 1

    def to_y(c, s):
        return c, s ^ 4

    def to_weights(c, s):
        return c, s ^ 2

    cell_list = sun_index.reshape(-1)
    features, xe_lo, xe_hi, ye_lo, ye_hi = pl.pallas_call(
        functools.partial(gather_kernel, cells, width_x, width_y),
        out_shape=(
            jax.ShapeDtypeStruct((capacity, fields, levels), BF16),
            jax.ShapeDtypeStruct((fields, WIDE, width_y, levels), BF16),
            jax.ShapeDtypeStruct((fields, WIDE, width_y, levels), BF16),
            jax.ShapeDtypeStruct((fields, WIDE, width_x, levels), BF16),
            jax.ShapeDtypeStruct((fields, WIDE, width_x, levels), BF16),
        ),
        in_specs=[smem(), smem(), vmem()],
        out_specs=(vmem(),) * 5,
        compiler_params=params(),
        name="gather_columns",
    )(cell_list, cos_zenith.reshape(-1), air_state.reshape(fields * cells, levels))

    table = jnp.concatenate(
        [out_bias[None, :], absorption[None, :], solar_flux[None, :], jnp.zeros((5, points), F32)], axis=0
    )
    features_z = send(features, to_z)
    other_weight = send(out_weight, to_weights)
    other_table = send(table, to_weights)
    xlo = send(xe_hi, lambda c, s: ((c + 1) % cols, s))
    xhi = send(xe_lo, lambda c, s: ((c - 1) % cols, s))
    mine = jnp.concatenate([features, features_z], axis=0)
    theirs = send(mine, to_y)

    rows_x = width_x + 2 * WIDE
    ym_lo, ym_hi = pl.pallas_call(
        edge_kernel,
        out_shape=(jax.ShapeDtypeStruct((fields, WIDE, rows_x, levels), BF16),) * 2,
        in_specs=[vmem()] * 4,
        out_specs=(vmem(),) * 2,
        scratch_shapes=[pltpu.VMEM((2 * WIDE * width_y, levels), F32)],
        compiler_params=params(),
        name="edge_rows",
    )(ye_lo, ye_hi, xlo, xhi)
    ylo = send(ym_hi, lambda c, s: (c, (s + 1) % spec))
    yhi = send(ym_lo, lambda c, s: (c, (s - 1) % spec))

    col_index, spec_index = lax.axis_index("cols"), lax.axis_index("spec")
    col_z = mirrored(col_index)
    counts = jnp.stack(
        [
            sun_count[spec_index, col_index],
            sun_count[spec_index ^ 1, col_z],
            sun_count[spec_index ^ 4, col_index],
            sun_count[spec_index ^ 5, col_z],
        ]
    )
    group_levels = LANES // fields
    half = (in_weight * 0.5).astype(BF16)
    half = jnp.concatenate([half, jnp.zeros((fields - NIN, hidden), BF16)], axis=0)
    place = jnp.arange(group_levels)
    take = place[None, :, None] == (2 * jnp.arange(group_levels // 2)[:, None, None] + jnp.arange(2)[None, None, :])
    first = jnp.where(
        take[:, None, :, :, None], half[None, :, None, None, :], jnp.zeros((), BF16)
    ).reshape(group_levels // 2, LANES, 2 * hidden)
    mid_half = (mid_weight * 0.5).astype(BF16)
    nothing = jnp.zeros_like(mid_half)
    mid = jnp.concatenate(
        [jnp.concatenate([mid_half, nothing], axis=1), jnp.concatenate([nothing, mid_half], axis=1)], axis=0
    )
    first_bias = jnp.tile(0.5 * in_bias, 2)[None, :]
    mid_bias2 = jnp.tile(0.5 * mid_bias, 2)[None, :]
    tables = jnp.concatenate([table[:3], other_table[:3]], axis=1)
    tables = jnp.broadcast_to(tables[:, :, None], (3, 2 * points, LANES))

    most_rows = 4 * capacity
    heat_mine, heat_theirs = pl.pallas_call(
        radiate_kernel,
        out_shape=(jax.ShapeDtypeStruct((2 * capacity, levels), F32),) * 2,
        in_specs=[smem()] + [vmem()] * 11,
        out_specs=(vmem(),) * 2,
        scratch_shapes=[
            pltpu.VMEM((most_rows * fields, levels), F32),
            pltpu.VMEM((levels // group_levels, LANES, LANES), BF16),
            pltpu.VMEM((levels, 2 * points, LANES), F32),
            pltpu.VMEM((levels * 8, LANES), F32),
            pltpu.VMEM((most_rows, levels), F32),
        ],
        compiler_params=params(),
        name="radiate",
    )(
        counts,
        mine,
        theirs,
        first,
        first_bias,
        mid,
        mid_bias2,
        out_weight,
        other_weight,
        tables[0],
        tables[1],
        tables[2],
    )
    heat_pair = heat_mine + send(heat_theirs, to_y)
    heat_z = send(heat_pair[capacity:], to_z)

    ax = 0.5 * courant_x * courant_x + DIFFUSION
    ay = 0.5 * courant_y * courant_y + DIFFUSION
    coefs = jnp.stack(
        [
            1.0 - 2.0 * ax - 2.0 * ay,
            ax - 0.5 * courant_x,
            ax + 0.5 * courant_x,
            ay - 0.5 * courant_y,
            ay + 0.5 * courant_y,
            ax,
            ax,
            ax,
        ]
    )
    x_spec = pl.BlockSpec((1, WIDE, width_y, levels), lambda f: (f, 0, 0, 0))
    y_spec = pl.BlockSpec((1, WIDE, rows_x, levels), lambda f: (f, 0, 0, 0))
    field_spec = pl.BlockSpec((1, cells, levels), lambda f: (f, 0, 0))
    rows_y = width_y + 2 * WIDE
    advected = pl.pallas_call(
        functools.partial(advect_kernel, width_x, width_y),
        grid=(fields,),
        out_shape=jax.ShapeDtypeStruct((fields, cells, levels), F32),
        in_specs=[field_spec, x_spec, x_spec, y_spec, y_spec, pl.BlockSpec((8, levels), lambda f: (0, 0))],
        out_specs=field_spec,
        scratch_shapes=[pltpu.VMEM((rows_x * rows_y, levels), F32)] * 2,
        compiler_params=params(),
        name="advect",
    )(air_state.reshape(fields, cells, levels), xlo, xhi, ylo, yhi, coefs)

    new_state, grid = pl.pallas_call(
        finish_kernel,
        out_shape=(
            jax.ShapeDtypeStruct((fields, cells, levels), F32),
            jax.ShapeDtypeStruct((cells, levels), F32),
        ),
        in_specs=[smem(), smem(), vmem(), vmem(), pl.BlockSpec(memory_space=pl.ANY)],
        out_specs=(pl.BlockSpec(memory_space=pl.ANY), vmem()),
        scratch_shapes=[pltpu.VMEM((cells, levels), F32), pltpu.SemaphoreType.DMA((2,))],
        input_output_aliases={4: 0},
        compiler_params=params(),
        name="finish",
    )(cell_list, counts, heat_pair[:capacity], heat_z, advected)
    return (
        new_state.reshape(fields, width_x, width_y, levels),
        grid.reshape(width_x, width_y, levels),
    )


def solution(mesh):
    placed = (
        P(None, "cols", "spec", None),
        P(),
        P(),
        P("cols", "spec"),
        P("cols", "spec", None),
        P(),
        P(),
        P(),
        P(),
        P(),
        P(None, "spec", None),
        P("spec"),
        P("spec"),
        P("spec"),
    )
    return jax.shard_map(
        on_device,
        mesh=mesh,
        in_specs=placed,
        out_specs=(P(None, "cols", "spec", None), P("cols", "spec", None)),
        check_vma=False,
    )
```

```python
import functools

import jax
import jax.numpy as jnp
from jax import lax
from jax.experimental import pallas as pl
from jax.experimental.pallas import tpu as pltpu
from jax.sharding import PartitionSpec as P

NIN = 7
SECTIONS = 4
WIDE = 4
DIFFUSION = 0.05
ALBEDO = 0.3
DIFFUSIVITY = 1.66
LANES = 128
LOG2E = 1.4426950408889634
MIB = 1024 * 1024

F32 = jnp.float32
BF16 = jnp.bfloat16


def vmem():
    return pl.BlockSpec(memory_space=pltpu.VMEM)


def smem():
    return pl.BlockSpec(memory_space=pltpu.SMEM)


def params(mib):
    return pltpu.CompilerParams(vmem_limit_bytes=mib * MIB)


def gather_kernel(cells, width_x, width_y, index_ref, cos_ref, state_ref, feat_ref, xlo_ref, xhi_ref, ylo_ref, yhi_ref):
    fields = state_ref.shape[0] // cells
    last = lax.broadcasted_iota(jnp.int32, (fields, LANES), 0) == NIN

    def one(j, carry):
        m = index_ref[j]
        rows = state_ref[pl.ds(m, fields, stride=cells), :]
        feat_ref[j] = jnp.where(last, cos_ref[m // width_y, m % width_y], rows).astype(BF16)
        return carry

    lax.fori_loop(0, feat_ref.shape[0], one, 0, unroll=8)
    for f in range(fields):
        for w in range(WIDE):
            xlo_ref[f, w] = state_ref[pl.ds(f * cells + w * width_y, width_y), :].astype(BF16)
            xhi_ref[f, w] = state_ref[pl.ds(f * cells + (width_x - WIDE + w) * width_y, width_y), :].astype(BF16)
            ylo_ref[f, w] = state_ref[pl.ds(f * cells + w, width_x, stride=width_y), :].astype(BF16)
            yhi_ref[f, w] = state_ref[pl.ds(f * cells + width_y - WIDE + w, width_x, stride=width_y), :].astype(BF16)


def edge_kernel(ylo_ref, yhi_ref, xlo_ref, xhi_ref, mlo_ref, mhi_ref, buf):
    width_y = xlo_ref.shape[2]
    for f in range(ylo_ref.shape[0]):
        for w in range(WIDE):
            buf[pl.ds(w * width_y, width_y), :] = xhi_ref[f, w].astype(F32)
            buf[pl.ds((WIDE + w) * width_y, width_y), :] = xlo_ref[f, w].astype(F32)
        for w in range(WIDE):
            for src, dst, row in ((ylo_ref, mlo_ref, w), (yhi_ref, mhi_ref, width_y - WIDE + w)):
                corner = buf[pl.ds(row, 2 * WIDE, stride=width_y), :]
                dst[f, w] = jnp.concatenate([src[f, w].astype(F32), corner], axis=0).astype(BF16)


def advect_kernel(width_x, width_y, state_ref, xlo_ref, xhi_ref, ylo_ref, yhi_ref, coef_ref, out_ref, one, two):
    ring_x, ring_y = width_x + 2 * WIDE, width_y + 2 * WIDE
    for x in range(width_x):
        one[pl.ds(x * ring_y, width_y), :] = state_ref[0, pl.ds(x * width_y, width_y), :]
    for w in range(WIDE):
        one[pl.ds((width_x + w) * ring_y, width_y), :] = xhi_ref[0, w].astype(F32)
        one[pl.ds((width_x + WIDE + w) * ring_y, width_y), :] = xlo_ref[0, w].astype(F32)
        one[pl.ds(width_y + w, ring_x, stride=ring_y), :] = yhi_ref[0, w].astype(F32)
        one[pl.ds(width_y + WIDE + w, ring_x, stride=ring_y), :] = ylo_ref[0, w].astype(F32)
    centre, east, west, north, south = (coef_ref[pl.ds(k, 1), :] for k in range(5))
    src, dst = one, two
    for section in range(SECTIONS):
        left = WIDE - 1 - section
        wanted = list(range(width_x + left)) + list(range(ring_x - left, ring_x))
        for x in wanted:
            q = src[pl.ds(x * ring_y, ring_y), :]
            e = src[pl.ds(((x + 1) % ring_x) * ring_y, ring_y), :]
            w = src[pl.ds(((x - 1) % ring_x) * ring_y, ring_y), :]
            n = pltpu.roll(q, ring_y - 1, 0)
            s = pltpu.roll(q, 1, 0)
            new = centre * q + east * e + west * w + north * n + south * s
            if section == SECTIONS - 1:
                out_ref[0, pl.ds(x * width_y, width_y), :] = new[:width_y]
            else:
                dst[pl.ds(x * ring_y, ring_y), :] = new
        src, dst = dst, src


def mirrored(c, cols):
    part = cols // 4
    return (3 - c // part) * part + c % part


def far(s, spec):
    return (spec // 2 - 1 - s // 2) * 2 + s % 2


def radiate_kernel(
    sun_ref,
    mine_ref,
    theirs_ref,
    first_ref,
    first_bias_ref,
    mid_ref,
    mid_bias_ref,
    outa_ref,
    outb_ref,
    out_bias_ref,
    absorb_ref,
    flux_ref,
    heat_mine_ref,
    heat_theirs_ref,
    packed,
    grouped,
    depths,
    sums,
    heats,
    hidden_one,
    hidden_two,
):
    capacity = mine_ref.shape[0] // 2
    levels = outa_ref.shape[0]
    points = absorb_ref.shape[0]
    fields = mine_ref.shape[1]
    group_levels = LANES // fields
    groups = levels // group_levels
    pairs = group_levels // 2
    sources = ((mine_ref, 0), (mine_ref, capacity), (theirs_ref, 0), (theirs_ref, capacity))
    spec, cols = sun_ref.shape
    c, s = lax.axis_index("cols"), lax.axis_index("spec")
    c_z, s_far = mirrored(c, cols), far(s, spec)
    near, away = s + 1 - 2 * (s % 2), s_far + 1 - 2 * (s % 2)
    counts = (sun_ref[s, c], sun_ref[near, c_z], sun_ref[s_far, c], sun_ref[away, c_z])
    offset = jnp.int32(0)
    offsets = []
    for t, (ref, base) in enumerate(sources):
        offsets.append(offset)

        def pack(i, carry, ref=ref, base=base, offset=offset):
            packed[pl.ds((offset + i) * fields, fields), :] = ref[base + i].astype(F32)
            return carry

        lax.fori_loop(0, counts[t], pack, 0)
        offset = offset + counts[t]
    lane = lax.broadcasted_iota(jnp.int32, (16, LANES), 1) // group_levels

    def chunk(q, carry):
        first_row = q * LANES

        def regroup(r, carry2):
            base = (first_row + r * 16) * fields
            rows = [packed[pl.ds(base + f, 16, stride=fields), :] for f in range(fields)]
            for g in range(groups):
                made = rows[0] if g == 0 else pltpu.roll(rows[0], (-g * group_levels) % LANES, 1)
                for f in range(1, fields):
                    shift = ((f - g) * group_levels) % LANES
                    moved = rows[f] if shift == 0 else pltpu.roll(rows[f], shift, 1)
                    made = jnp.where(lane == f, moved, made)
                grouped[g, pl.ds(pl.multiple_of(r * 16, 16), 16), :] = made.astype(BF16)
            return carry2

        lax.fori_loop(0, LANES // 16, regroup, 0)
        slant_rows = packed[pl.ds(first_row * fields + NIN, LANES, stride=fields), :]
        cosine = jnp.transpose(slant_rows)[:8, :]

        def stage_one(i):
            u = jnp.dot(grouped[i // pairs], first_ref[i % pairs], preferred_element_type=F32) + first_bias_ref[...]
            hidden_one[...] = (u + u * jnp.tanh(u)).astype(BF16)

        def stage_two():
            v = jnp.dot(hidden_one[...], mid_ref[...], preferred_element_type=F32) + mid_bias_ref[...]
            hidden_two[...] = (v + v * jnp.tanh(v)).astype(BF16)

        def stage_three(i, depth):
            for j in range(2):
                level = 2 * i + j
                weight = jnp.concatenate([outa_ref[level], outb_ref[level]], axis=0)
                logits = lax.dot_general(
                    weight,
                    hidden_two[:, j * LANES : (j + 1) * LANES],
                    (((1,), (1,)), ((), ())),
                    preferred_element_type=F32,
                )
                logits = logits + out_bias_ref[...]
                soft = jnp.maximum(logits, 0.0) + jnp.log(1.0 + jnp.exp2(-LOG2E * jnp.abs(logits)))
                depth = depth + absorb_ref[...] * soft
                depths[level] = depth
            return depth

        steps = levels // 2
        stage_one(0)
        stage_two()
        stage_one(1)

        def step(i, depth):
            depth = stage_three(i, depth)
            stage_two()
            stage_one(jnp.minimum(i + 2, steps - 1))
            return depth

        total = lax.fori_loop(0, steps, step, jnp.zeros((points, LANES), F32))
        wide = jnp.tile(cosine, (points // 8, 1))
        source = flux_ref[...] * wide
        steep = -LOG2E / wide
        down_log = jnp.log(source) * LOG2E
        up_log = jnp.log(ALBEDO * source) * LOG2E + total * (steep - LOG2E * DIFFUSIVITY)
        before = source - jnp.exp2(up_log)

        def level_heat(level, before):
            depth = depths[level]
            now = jnp.exp2(depth * steep + down_log) - jnp.exp2(depth * (LOG2E * DIFFUSIVITY) + up_log)
            lost = before - now
            sums[pl.ds(pl.multiple_of(level * 8, 8), 8), :] = jnp.sum(lost.reshape(points // 8, 8, LANES), axis=0)
            return now

        lax.fori_loop(0, levels, level_heat, before, unroll=2)
        heat = sums[pl.ds(0, levels, stride=8), :]
        for k in range(1, 8):
            heat = heat + sums[pl.ds(k, levels, stride=8), :]
        heats[pl.ds(pl.multiple_of(first_row, LANES), LANES), :] = jnp.transpose(heat)
        return carry

    lax.fori_loop(0, (offset + LANES - 1) // LANES, chunk, 0)
    for t, (ref, base) in enumerate(
        ((heat_mine_ref, 0), (heat_mine_ref, capacity), (heat_theirs_ref, 0), (heat_theirs_ref, capacity))
    ):

        def unpack(i, carry, ref=ref, base=base, offset=offsets[t]):
            ref[pl.ds(base + i, 1), :] = heats[pl.ds(offset + i, 1), :]
            return carry

        lax.fori_loop(0, counts[t], unpack, 0)


def finish_kernel(index_ref, sun_ref, heat_a, heat_b, state_in, state_out, grid_ref, plane, sems):
    fetch = pltpu.make_async_copy(state_in.at[0], plane, sems.at[0])
    fetch.start()
    grid_ref[...] = jnp.zeros_like(grid_ref)

    def one(j, carry):
        grid_ref[pl.ds(index_ref[j], 1), :] = heat_a[pl.ds(j, 1), :] + heat_b[pl.ds(j, 1), :]
        return carry

    lax.fori_loop(0, sun_ref[lax.axis_index("spec"), lax.axis_index("cols")], one, 0)
    fetch.wait()
    plane[...] = plane[...] + grid_ref[...]
    store = pltpu.make_async_copy(plane, state_out.at[0], sems.at[1])
    store.start()
    store.wait()


def on_device(
    air_state,
    courant_x,
    courant_y,
    cos_zenith,
    sun_index,
    sun_count,
    in_weight,
    in_bias,
    mid_weight,
    mid_bias,
    out_weight,
    out_bias,
    absorption,
    solar_flux,
):
    fields, width_x, width_y, levels = air_state.shape
    cells = width_x * width_y
    capacity = sun_index.shape[-1]
    hidden = mid_weight.shape[0]
    points = out_weight.shape[1]
    cols, spec = lax.axis_size("cols"), lax.axis_size("spec")
    def both(target):
        return [(c * spec + s, (lambda d: d[0] * spec + d[1])(target(c, s))) for c in range(cols) for s in range(spec)]

    def send(value, target):
        return lax.ppermute(value, ("cols", "spec"), both(target))

    def to_z(c, s):
        return mirrored(c, cols), s ^ 1

    def to_y(c, s):
        return c, far(s, spec)

    def to_weights(c, s):
        return c, s ^ 2

    cell_list = sun_index.reshape(-1)
    features, xe_lo, xe_hi, ye_lo, ye_hi = pl.pallas_call(
        functools.partial(gather_kernel, cells, width_x, width_y),
        out_shape=(
            jax.ShapeDtypeStruct((capacity, fields, levels), BF16),
            jax.ShapeDtypeStruct((fields, WIDE, width_y, levels), BF16),
            jax.ShapeDtypeStruct((fields, WIDE, width_y, levels), BF16),
            jax.ShapeDtypeStruct((fields, WIDE, width_x, levels), BF16),
            jax.ShapeDtypeStruct((fields, WIDE, width_x, levels), BF16),
        ),
        in_specs=[smem(), smem(), vmem()],
        out_specs=(vmem(),) * 5,
        compiler_params=params(14),
        name="gather_columns",
    )(cell_list, cos_zenith, air_state.reshape(fields * cells, levels))

    table = jnp.concatenate(
        [out_bias[None, :], absorption[None, :], solar_flux[None, :], jnp.zeros((5, points), F32)], axis=0
    )
    features_z = send(features, to_z)
    other_weight = send(out_weight, to_weights)
    other_table = send(table, to_weights)
    xlo = send(xe_hi, lambda c, s: ((c + 1) % cols, s))
    xhi = send(xe_lo, lambda c, s: ((c - 1) % cols, s))
    mine = jnp.concatenate([features, features_z], axis=0)

    mine, in_weight, in_bias, mid_weight, mid_bias, courant_x, courant_y = lax.optimization_barrier(
        (mine, in_weight, in_bias, mid_weight, mid_bias, courant_x, courant_y)
    )
    theirs = send(mine, to_y)
    rows_x = width_x + 2 * WIDE
    ym_lo, ym_hi = pl.pallas_call(
        edge_kernel,
        out_shape=(jax.ShapeDtypeStruct((fields, WIDE, rows_x, levels), BF16),) * 2,
        in_specs=[vmem()] * 4,
        out_specs=(vmem(),) * 2,
        scratch_shapes=[pltpu.VMEM((2 * WIDE * width_y, levels), F32)],
        compiler_params=params(6),
        name="edge_rows",
    )(ye_lo, ye_hi, xlo, xhi)
    mine, ym_lo, ym_hi = lax.optimization_barrier((mine, ym_lo, ym_hi))
    ylo = send(ym_hi, lambda c, s: (c, (s + 1) % spec))
    yhi = send(ym_lo, lambda c, s: (c, (s - 1) % spec))

    group_levels = LANES // fields
    half = (in_weight * 0.5).astype(BF16)
    half = jnp.concatenate([half, jnp.zeros((fields - NIN, hidden), BF16)], axis=0)
    place = jnp.arange(group_levels)
    take = place[None, :, None] == (2 * jnp.arange(group_levels // 2)[:, None, None] + jnp.arange(2)[None, None, :])
    first = jnp.where(
        take[:, None, :, :, None], half[None, :, None, None, :], jnp.zeros((), BF16)
    ).reshape(group_levels // 2, LANES, 2 * hidden)
    mid_half = (mid_weight * 0.5).astype(BF16)
    nothing = jnp.zeros_like(mid_half)
    mid = jnp.concatenate(
        [jnp.concatenate([mid_half, nothing], axis=1), jnp.concatenate([nothing, mid_half], axis=1)], axis=0
    )
    first_bias = jnp.tile(0.5 * in_bias, 2)[None, :]
    mid_bias2 = jnp.tile(0.5 * mid_bias, 2)[None, :]
    tables = jnp.concatenate([table[:3], other_table[:3]], axis=1)
    tables = jnp.broadcast_to(tables[:, :, None], (3, 2 * points, LANES))

    most_rows = 4 * capacity
    heat_mine, heat_theirs = pl.pallas_call(
        radiate_kernel,
        out_shape=(jax.ShapeDtypeStruct((2 * capacity, levels), F32),) * 2,
        in_specs=[smem()] + [vmem()] * 11,
        out_specs=(vmem(),) * 2,
        scratch_shapes=[
            pltpu.VMEM((most_rows * fields, levels), F32),
            pltpu.VMEM((levels // group_levels, LANES, LANES), BF16),
            pltpu.VMEM((levels, 2 * points, LANES), F32),
            pltpu.VMEM((levels * 8, LANES), F32),
            pltpu.VMEM((most_rows, levels), F32),
            pltpu.VMEM((LANES, 2 * hidden), BF16),
            pltpu.VMEM((LANES, 2 * hidden), BF16),
        ],
        compiler_params=params(20),
        cost_estimate=pl.CostEstimate(flops=2 * 10**10, bytes_accessed=4 * 10**6, transcendentals=10**7),
        name="radiate",
    )(
        sun_count,
        mine,
        theirs,
        first,
        first_bias,
        mid,
        mid_bias2,
        out_weight,
        other_weight,
        tables[0],
        tables[1],
        tables[2],
    )
    heat_back = send(heat_theirs, to_y)

    ax = 0.5 * courant_x * courant_x + DIFFUSION
    ay = 0.5 * courant_y * courant_y + DIFFUSION
    coefs = jnp.stack(
        [
            1.0 - 2.0 * ax - 2.0 * ay,
            ax - 0.5 * courant_x,
            ax + 0.5 * courant_x,
            ay - 0.5 * courant_y,
            ay + 0.5 * courant_y,
            ax,
            ax,
            ax,
        ]
    )
    rows_y = width_y + 2 * WIDE
    def advance(first_field, count, earlier):
        def block(shape):
            return pl.BlockSpec((1,) + shape, lambda f: (first_field + f,) + (0,) * len(shape))

        x_spec, y_spec, field_spec = block((WIDE, width_y, levels)), block((WIDE, rows_x, levels)), block((cells, levels))
        kernel = functools.partial(advect_kernel, width_x, width_y)
        given = [air_state.reshape(fields, cells, levels), xlo, xhi, ylo, yhi, coefs]
        specs = [field_spec, x_spec, x_spec, y_spec, y_spec, pl.BlockSpec((8, levels), lambda f: (0, 0))]
        aliases = {}
        if earlier is not None:
            given, specs, aliases = [earlier] + given, [pl.BlockSpec(memory_space=pl.ANY)] + specs, {0: 0}
            kernel = functools.partial(lambda inner, unused, *refs: inner(*refs), kernel)
        return pl.pallas_call(
            kernel,
            grid=(count,),
            out_shape=jax.ShapeDtypeStruct((fields, cells, levels), F32),
            in_specs=specs,
            out_specs=field_spec,
            scratch_shapes=[pltpu.VMEM((rows_x * rows_y, levels), F32)] * 2,
            input_output_aliases=aliases,
            compiler_params=params(6),
            cost_estimate=pl.CostEstimate(flops=4 * 10**9, bytes_accessed=8 * 10**6, transcendentals=0),
            name="advect",
        )(*given)

    half_way = advance(0, fields // 2, None)
    half_way, heat_back = lax.optimization_barrier((half_way, heat_back))
    heat_pair = heat_mine + heat_back
    heat_z = send(heat_pair[capacity:], to_z)
    advected = advance(fields // 2, fields // 2, half_way)

    new_state, grid = pl.pallas_call(
        finish_kernel,
        out_shape=(
            jax.ShapeDtypeStruct((fields, cells, levels), F32),
            jax.ShapeDtypeStruct((cells, levels), F32),
        ),
        in_specs=[smem(), smem(), vmem(), vmem(), pl.BlockSpec(memory_space=pl.ANY)],
        out_specs=(pl.BlockSpec(memory_space=pl.ANY), vmem()),
        scratch_shapes=[pltpu.VMEM((cells, levels), F32), pltpu.SemaphoreType.DMA((2,))],
        input_output_aliases={4: 0},
        compiler_params=params(4),
        name="finish",
    )(cell_list, sun_count, heat_pair[:capacity], heat_z, advected)
    return (
        new_state.reshape(fields, width_x, width_y, levels),
        grid.reshape(width_x, width_y, levels),
    )


def solution(mesh):
    placed = (
        P(None, "cols", "spec", None),
        P(),
        P(),
        P("cols", "spec"),
        P("cols", "spec", None),
        P(),
        P(),
        P(),
        P(),
        P(),
        P(None, "spec", None),
        P("spec"),
        P("spec"),
        P("spec"),
    )
    return jax.shard_map(
        on_device,
        mesh=mesh,
        in_specs=placed,
        out_specs=(P(None, "cols", "spec", None), P("cols", "spec", None)),
        check_vma=False,
    )
```

```python
import functools

import jax
import jax.numpy as jnp
from jax import lax
from jax.experimental import pallas as pl
from jax.experimental.pallas import tpu as pltpu
from jax.sharding import PartitionSpec as P

NIN = 7
SECTIONS = 4
WIDE = 4
DIFFUSION = 0.05
ALBEDO = 0.3
DIFFUSIVITY = 1.66
LANES = 128
BESIDE = 4
LOG2E = 1.4426950408889634
MIB = 1024 * 1024

F32 = jnp.float32
BF16 = jnp.bfloat16


def vmem():
    return pl.BlockSpec(memory_space=pltpu.VMEM)


def smem():
    return pl.BlockSpec(memory_space=pltpu.SMEM)


def params(mib):
    return pltpu.CompilerParams(vmem_limit_bytes=mib * MIB)


def gather_kernel(cells, width_x, width_y, index_ref, cos_ref, state_ref, feat_ref, xlo_ref, xhi_ref, ylo_ref, yhi_ref):
    fields = state_ref.shape[0] // cells
    last = lax.broadcasted_iota(jnp.int32, (fields, LANES), 0) == NIN

    def one(j, carry):
        m = index_ref[j]
        rows = state_ref[pl.ds(m, fields, stride=cells), :]
        feat_ref[j] = jnp.where(last, cos_ref[m // width_y, m % width_y], rows).astype(BF16)
        return carry

    lax.fori_loop(0, feat_ref.shape[0], one, 0, unroll=8)
    for f in range(fields):
        for w in range(WIDE):
            xlo_ref[f, w] = state_ref[pl.ds(f * cells + w * width_y, width_y), :].astype(BF16)
            xhi_ref[f, w] = state_ref[pl.ds(f * cells + (width_x - WIDE + w) * width_y, width_y), :].astype(BF16)
            ylo_ref[f, w] = state_ref[pl.ds(f * cells + w, width_x, stride=width_y), :].astype(BF16)
            yhi_ref[f, w] = state_ref[pl.ds(f * cells + width_y - WIDE + w, width_x, stride=width_y), :].astype(BF16)


def edge_kernel(ylo_ref, yhi_ref, xlo_ref, xhi_ref, mlo_ref, mhi_ref, buf):
    width_y = xlo_ref.shape[2]
    for f in range(ylo_ref.shape[0]):
        for w in range(WIDE):
            buf[pl.ds(w * width_y, width_y), :] = xhi_ref[f, w].astype(F32)
            buf[pl.ds((WIDE + w) * width_y, width_y), :] = xlo_ref[f, w].astype(F32)
        for w in range(WIDE):
            for src, dst, row in ((ylo_ref, mlo_ref, w), (yhi_ref, mhi_ref, width_y - WIDE + w)):
                corner = buf[pl.ds(row, 2 * WIDE, stride=width_y), :]
                dst[f, w] = jnp.concatenate([src[f, w].astype(F32), corner], axis=0).astype(BF16)


def weights_kernel(
    in_ref, in_bias_ref, mid_in_ref, mid_bias_in_ref, table_ref, other_ref, first_ref, first_bias_ref, mid_ref, mid_bias_ref, spread_ref
):
    hidden = mid_in_ref.shape[0]
    points = spread_ref.shape[1] // 2
    group_levels = 2 * first_ref.shape[0]
    half = in_ref[...].astype(F32) * 0.5
    rows = [jnp.broadcast_to(half[f : f + 1], (group_levels, hidden)) for f in range(NIN)]
    rows.append(jnp.zeros((LANES - NIN * group_levels, hidden), F32))
    spread = jnp.concatenate(rows, axis=0)
    place = lax.broadcasted_iota(jnp.int32, (LANES, hidden), 0) % group_levels
    for p in range(group_levels // 2):
        for j in range(2):
            first_ref[p, :, j * hidden : (j + 1) * hidden] = jnp.where(place == 2 * p + j, spread, 0.0).astype(BF16)
    mid = (mid_in_ref[...].astype(F32) * 0.5).astype(BF16)
    nothing = jnp.zeros_like(mid)
    mid_ref[:hidden, :hidden] = mid
    mid_ref[:hidden, hidden:] = nothing
    mid_ref[hidden:, :hidden] = nothing
    mid_ref[hidden:, hidden:] = mid
    for src, dst in ((in_bias_ref, first_bias_ref), (mid_bias_in_ref, mid_bias_ref)):
        dst[:, :hidden] = src[...] * 0.5
        dst[:, hidden:] = src[...] * 0.5
    for k in range(3):
        for src, at in ((table_ref, 0), (other_ref, points)):
            row = jnp.broadcast_to(src[k : k + 1, :], (LANES, LANES))
            spread_ref[k, at : at + points, :] = jnp.transpose(row)[:points, :]


def advect_kernel(width_x, width_y, state_ref, xlo_ref, xhi_ref, ylo_ref, yhi_ref, cx_ref, cy_ref, out_ref, one, two):
    ring_x, ring_y = width_x + 2 * WIDE, width_y + 2 * WIDE
    for x in range(width_x):
        one[pl.ds(x * ring_y, width_y), :] = state_ref[0, pl.ds(x * width_y, width_y), :]
    for w in range(WIDE):
        one[pl.ds((width_x + w) * ring_y, width_y), :] = xhi_ref[0, w].astype(F32)
        one[pl.ds((width_x + WIDE + w) * ring_y, width_y), :] = xlo_ref[0, w].astype(F32)
        one[pl.ds(width_y + w, ring_x, stride=ring_y), :] = yhi_ref[0, w].astype(F32)
        one[pl.ds(width_y + WIDE + w, ring_x, stride=ring_y), :] = ylo_ref[0, w].astype(F32)
    cx, cy = cx_ref[...], cy_ref[...]
    ax = 0.5 * cx * cx + DIFFUSION
    ay = 0.5 * cy * cy + DIFFUSION
    centre, east, west, north, south = 1.0 - 2.0 * ax - 2.0 * ay, ax - 0.5 * cx, ax + 0.5 * cx, ay - 0.5 * cy, ay + 0.5 * cy
    src, dst = one, two
    for section in range(SECTIONS):
        left = WIDE - 1 - section
        wanted = list(range(width_x + left)) + list(range(ring_x - left, ring_x))
        for x in wanted:
            q = src[pl.ds(x * ring_y, ring_y), :]
            e = src[pl.ds(((x + 1) % ring_x) * ring_y, ring_y), :]
            w = src[pl.ds(((x - 1) % ring_x) * ring_y, ring_y), :]
            n = pltpu.roll(q, ring_y - 1, 0)
            s = pltpu.roll(q, 1, 0)
            new = centre * q + east * e + west * w + north * n + south * s
            if section == SECTIONS - 1:
                out_ref[0, pl.ds(x * width_y, width_y), :] = new[:width_y]
            else:
                dst[pl.ds(x * ring_y, ring_y), :] = new
        src, dst = dst, src


def mirrored(c, cols):
    part = cols // 4
    return (3 - c // part) * part + c % part


def far(s, spec):
    return (spec // 2 - 1 - s // 2) * 2 + s % 2


def radiate_kernel(
    sun_ref,
    own_ref,
    z_ref,
    far_ref,
    far_z_ref,
    first_ref,
    first_bias_ref,
    mid_ref,
    mid_bias_ref,
    outa_ref,
    outb_ref,
    spread_ref,
    heat_mine_ref,
    heat_theirs_ref,
    packed,
    grouped,
    depths,
    sums,
    heats,
    hidden_one,
    hidden_two,
):
    capacity = own_ref.shape[0]
    levels = outa_ref.shape[0]
    points = spread_ref.shape[1]
    fields = own_ref.shape[1]
    group_levels = LANES // fields
    groups = levels // group_levels
    pairs = group_levels // 2
    sources = (own_ref, z_ref, far_ref, far_z_ref)
    spec, cols = sun_ref.shape
    c, s = lax.axis_index("cols"), lax.axis_index("spec")
    c_z, s_far = mirrored(c, cols), far(s, spec)
    near, away = s + 1 - 2 * (s % 2), s_far + 1 - 2 * (s % 2)
    counts = (sun_ref[s, c], sun_ref[near, c_z], sun_ref[s_far, c], sun_ref[away, c_z])
    offset = jnp.int32(0)
    offsets = []
    for t, ref in enumerate(sources):
        offsets.append(offset)

        def pack(i, carry, ref=ref, offset=offset):
            packed[pl.ds((offset + i) * fields, fields), :] = ref[i].astype(F32)
            return carry

        lax.fori_loop(0, counts[t], pack, 0)
        offset = offset + counts[t]
    lane = lax.broadcasted_iota(jnp.int32, (16, LANES), 1) // group_levels

    def chunk(q, carry):
        first_row = q * LANES

        def regroup(r, carry2):
            base = (first_row + r * 16) * fields
            rows = [packed[pl.ds(base + f, 16, stride=fields), :] for f in range(fields)]
            for g in range(groups):
                made = rows[0] if g == 0 else pltpu.roll(rows[0], (-g * group_levels) % LANES, 1)
                for f in range(1, fields):
                    shift = ((f - g) * group_levels) % LANES
                    moved = rows[f] if shift == 0 else pltpu.roll(rows[f], shift, 1)
                    made = jnp.where(lane == f, moved, made)
                grouped[g, pl.ds(pl.multiple_of(r * 16, 16), 16), :] = made.astype(BF16)
            return carry2

        lax.fori_loop(0, LANES // 16, regroup, 0, unroll=2)
        slant_rows = packed[pl.ds(first_row * fields + NIN, LANES, stride=fields), :]
        cosine = jnp.transpose(slant_rows)[:8, :]

        def stage_one(i):
            for t in range(BESIDE):
                k = i * BESIDE + t
                u = jnp.dot(grouped[k // pairs], first_ref[k % pairs], preferred_element_type=F32) + first_bias_ref[...]
                hidden_one[t] = (u + u * jnp.tanh(u)).astype(BF16)

        def stage_two():
            for t in range(BESIDE):
                v = jnp.dot(hidden_one[t], mid_ref[...], preferred_element_type=F32) + mid_bias_ref[...]
                hidden_two[t] = (v + v * jnp.tanh(v)).astype(BF16)

        def stage_three(i, depth):
            for t in range(BESIDE):
                for j in range(2):
                    level = 2 * (i * BESIDE + t) + j
                    weight = jnp.concatenate([outa_ref[level], outb_ref[level]], axis=0)
                    logits = lax.dot_general(
                        weight,
                        hidden_two[t, :, j * LANES : (j + 1) * LANES],
                        (((1,), (1,)), ((), ())),
                        preferred_element_type=F32,
                    )
                    logits = logits + spread_ref[0]
                    soft = jnp.maximum(logits, 0.0) + jnp.log(1.0 + jnp.exp2(-LOG2E * jnp.abs(logits)))
                    depth = depth + spread_ref[1] * soft
                    depths[level] = depth
            return depth

        steps = levels // (2 * BESIDE)
        stage_one(0)
        stage_two()
        stage_one(1)

        def step(i, depth):
            depth = stage_three(i, depth)
            stage_two()
            stage_one(jnp.minimum(i + 2, steps - 1))
            return depth

        total = lax.fori_loop(0, steps, step, jnp.zeros((points, LANES), F32))
        wide = jnp.tile(cosine, (points // 8, 1))
        source = spread_ref[2] * wide
        steep = -LOG2E / wide
        down_log = jnp.log(source) * LOG2E
        up_log = jnp.log(ALBEDO * source) * LOG2E + total * (steep - LOG2E * DIFFUSIVITY)
        before = source - jnp.exp2(up_log)

        def level_heat(level, before):
            depth = depths[level]
            now = jnp.exp2(depth * steep + down_log) - jnp.exp2(depth * (LOG2E * DIFFUSIVITY) + up_log)
            lost = before - now
            sums[pl.ds(pl.multiple_of(level * 8, 8), 8), :] = jnp.sum(lost.reshape(points // 8, 8, LANES), axis=0)
            return now

        lax.fori_loop(0, levels, level_heat, before, unroll=4)
        heat = sums[pl.ds(0, levels, stride=8), :]
        for k in range(1, 8):
            heat = heat + sums[pl.ds(k, levels, stride=8), :]
        heats[pl.ds(pl.multiple_of(first_row, LANES), LANES), :] = jnp.transpose(heat)
        return carry

    lax.fori_loop(0, (offset + LANES - 1) // LANES, chunk, 0)
    for t, (ref, base) in enumerate(
        ((heat_mine_ref, 0), (heat_mine_ref, capacity), (heat_theirs_ref, 0), (heat_theirs_ref, capacity))
    ):

        def unpack(i, carry, ref=ref, base=base, offset=offsets[t]):
            ref[pl.ds(base + i, 1), :] = heats[pl.ds(offset + i, 1), :]
            return carry

        lax.fori_loop(0, counts[t], unpack, 0)


def finish_kernel(index_ref, sun_ref, heat_a, heat_b, state_in, state_out, grid_out, grid, plane, sems):
    fetch = pltpu.make_async_copy(state_in.at[0], plane, sems.at[0])
    fetch.start()
    grid[...] = jnp.zeros_like(grid)

    def one(j, carry):
        grid[pl.ds(index_ref[j], 1), :] = heat_a[pl.ds(j, 1), :] + heat_b[pl.ds(j, 1), :]
        return carry

    lax.fori_loop(0, sun_ref[lax.axis_index("spec"), lax.axis_index("cols")], one, 0)
    keep = pltpu.make_async_copy(grid, grid_out, sems.at[1])
    keep.start()
    fetch.wait()
    plane[...] = plane[...] + grid[...]
    store = pltpu.make_async_copy(plane, state_out.at[0], sems.at[2])
    store.start()
    keep.wait()
    store.wait()


def on_device(
    air_state,
    courant_x,
    courant_y,
    cos_zenith,
    sun_index,
    sun_count,
    in_weight,
    in_bias,
    mid_weight,
    mid_bias,
    out_weight,
    out_bias,
    absorption,
    solar_flux,
):
    fields, width_x, width_y, levels = air_state.shape
    cells = width_x * width_y
    capacity = sun_index.shape[-1]
    hidden = mid_weight.shape[0]
    points = out_weight.shape[1]
    cols, spec = lax.axis_size("cols"), lax.axis_size("spec")
    def both(target):
        return [(c * spec + s, (lambda d: d[0] * spec + d[1])(target(c, s))) for c in range(cols) for s in range(spec)]

    def send(value, target):
        return lax.ppermute(value, ("cols", "spec"), both(target))

    def to_z(c, s):
        return mirrored(c, cols), s ^ 1

    def to_y(c, s):
        return c, far(s, spec)

    def to_weights(c, s):
        return c, s ^ 2

    with jax.named_scope("send_weights"):
        other_weight = send(out_weight, to_weights)
    cell_list = sun_index.reshape(-1)
    features, xe_lo, xe_hi, ye_lo, ye_hi = pl.pallas_call(
        functools.partial(gather_kernel, cells, width_x, width_y),
        out_shape=(
            jax.ShapeDtypeStruct((capacity, fields, levels), BF16),
            jax.ShapeDtypeStruct((fields, WIDE, width_y, levels), BF16),
            jax.ShapeDtypeStruct((fields, WIDE, width_y, levels), BF16),
            jax.ShapeDtypeStruct((fields, WIDE, width_x, levels), BF16),
            jax.ShapeDtypeStruct((fields, WIDE, width_x, levels), BF16),
        ),
        in_specs=[smem(), smem(), vmem()],
        out_specs=(vmem(),) * 5,
        compiler_params=params(14),
        name="gather_columns",
    )(cell_list, cos_zenith, air_state.reshape(fields * cells, levels))

    with jax.named_scope("send_z"):
        features_z = send(features, to_z)
    with jax.named_scope("send_far"):
        features_far = send(features, to_y)
    with jax.named_scope("send_x"):
        xlo = send(xe_hi, lambda c, s: ((c + 1) % cols, s))
        xhi = send(xe_lo, lambda c, s: ((c - 1) % cols, s))
    out_bias, absorption, solar_flux, _ = lax.optimization_barrier((out_bias, absorption, solar_flux, features))
    table = jnp.stack([out_bias, absorption, solar_flux])
    table = jnp.pad(table, ((0, 5), (0, LANES - points)))
    with jax.named_scope("send_table"):
        other_table = send(table, to_weights)
    with jax.named_scope("send_far_z"):
        features_far_z = send(features_z, to_y)

    rows_x, rows_y = width_x + 2 * WIDE, width_y + 2 * WIDE
    xlo, xhi, features_z = lax.optimization_barrier((xlo, xhi, features_z))
    with jax.named_scope("edges"):
        ym_lo, ym_hi = pl.pallas_call(
            edge_kernel,
            out_shape=(jax.ShapeDtypeStruct((fields, WIDE, rows_x, levels), BF16),) * 2,
            in_specs=[vmem()] * 4,
            out_specs=(vmem(),) * 2,
            scratch_shapes=[pltpu.VMEM((2 * WIDE * width_y, levels), F32)],
            compiler_params=params(6),
            name="edge_rows",
        )(ye_lo, ye_hi, xlo, xhi)
    features_z, ym_lo, ym_hi = lax.optimization_barrier((features_z, ym_lo, ym_hi))
    with jax.named_scope("send_y"):
        ylo = send(ym_hi, lambda c, s: (c, (s + 1) % spec))
        yhi = send(ym_lo, lambda c, s: (c, (s - 1) % spec))

    group_levels = LANES // fields
    first, first_bias, mid, mid_bias2, spread = pl.pallas_call(
        weights_kernel,
        out_shape=(
            jax.ShapeDtypeStruct((group_levels // 2, LANES, 2 * hidden), BF16),
            jax.ShapeDtypeStruct((1, 2 * hidden), F32),
            jax.ShapeDtypeStruct((2 * hidden, 2 * hidden), BF16),
            jax.ShapeDtypeStruct((1, 2 * hidden), F32),
            jax.ShapeDtypeStruct((3, 2 * points, LANES), F32),
        ),
        in_specs=[vmem()] * 6,
        out_specs=(vmem(),) * 5,
        compiler_params=params(4),
        name="layer_weights",
    )(in_weight, in_bias[None, :], mid_weight, mid_bias[None, :], table, other_table)

    most_rows = 4 * capacity
    heat_mine, heat_theirs = pl.pallas_call(
        radiate_kernel,
        out_shape=(jax.ShapeDtypeStruct((2 * capacity, levels), F32),) * 2,
        in_specs=[smem()] + [vmem()] * 11,
        out_specs=(vmem(),) * 2,
        scratch_shapes=[
            pltpu.VMEM((most_rows * fields, levels), F32),
            pltpu.VMEM((levels // group_levels, LANES, LANES), BF16),
            pltpu.VMEM((levels, 2 * points, LANES), F32),
            pltpu.VMEM((levels * 8, LANES), F32),
            pltpu.VMEM((most_rows, levels), F32),
            pltpu.VMEM((BESIDE, LANES, 2 * hidden), BF16),
            pltpu.VMEM((BESIDE, LANES, 2 * hidden), BF16),
        ],
        compiler_params=params(20),
        cost_estimate=pl.CostEstimate(flops=2 * 10**10, bytes_accessed=4 * 10**6, transcendentals=10**7),
        name="radiate",
    )(
        sun_count,
        features,
        features_z,
        features_far,
        features_far_z,
        first,
        first_bias,
        mid,
        mid_bias2,
        out_weight,
        other_weight,
        spread,
    )
    heat_back = send(heat_theirs, to_y)

    def advance(first_field, count, earlier):
        def block(shape):
            return pl.BlockSpec((1,) + shape, lambda f: (first_field + f,) + (0,) * len(shape))

        x_spec, y_spec, field_spec = block((WIDE, width_y, levels)), block((WIDE, rows_x, levels)), block((cells, levels))
        kernel = functools.partial(advect_kernel, width_x, width_y)
        given = [air_state.reshape(fields, cells, levels), xlo, xhi, ylo, yhi, courant_x[None, :], courant_y[None, :]]
        specs = [field_spec, x_spec, x_spec, y_spec, y_spec] + [pl.BlockSpec((1, levels), lambda f: (0, 0))] * 2
        aliases = {}
        if earlier is not None:
            given, specs, aliases = [earlier] + given, [pl.BlockSpec(memory_space=pl.ANY)] + specs, {0: 0}
            kernel = functools.partial(lambda inner, unused, *refs: inner(*refs), kernel)
        return pl.pallas_call(
            kernel,
            grid=(count,),
            out_shape=jax.ShapeDtypeStruct((fields, cells, levels), F32),
            in_specs=specs,
            out_specs=field_spec,
            scratch_shapes=[pltpu.VMEM((rows_x * rows_y, levels), F32)] * 2,
            input_output_aliases=aliases,
            compiler_params=params(6),
            cost_estimate=pl.CostEstimate(flops=4 * 10**9, bytes_accessed=8 * 10**6, transcendentals=0),
            name="advect",
        )(*given)

    half_way = advance(0, fields // 2, None)
    half_way, heat_back = lax.optimization_barrier((half_way, heat_back))
    heat_pair = heat_mine + heat_back
    heat_z = send(heat_pair[capacity:], to_z)
    advected = advance(fields // 2, fields // 2, half_way)

    new_state, grid = pl.pallas_call(
        finish_kernel,
        out_shape=(
            jax.ShapeDtypeStruct((fields, cells, levels), F32),
            jax.ShapeDtypeStruct((cells, levels), F32),
        ),
        in_specs=[smem(), smem(), vmem(), vmem(), pl.BlockSpec(memory_space=pl.ANY)],
        out_specs=(pl.BlockSpec(memory_space=pl.ANY),) * 2,
        scratch_shapes=[pltpu.VMEM((cells, levels), F32)] * 2 + [pltpu.SemaphoreType.DMA((3,))],
        input_output_aliases={4: 0},
        compiler_params=params(4),
        name="finish",
    )(cell_list, sun_count, heat_pair[:capacity], heat_z, advected)
    return (
        new_state.reshape(fields, width_x, width_y, levels),
        grid.reshape(width_x, width_y, levels),
    )


def solution(mesh):
    placed = (
        P(None, "cols", "spec", None),
        P(),
        P(),
        P("cols", "spec"),
        P("cols", "spec", None),
        P(),
        P(),
        P(),
        P(),
        P(),
        P(None, "spec", None),
        P("spec"),
        P("spec"),
        P("spec"),
    )
    return jax.shard_map(
        on_device,
        mesh=mesh,
        in_specs=placed,
        out_specs=(P(None, "cols", "spec", None), P("cols", "spec", None)),
        check_vma=False,
    )
```
